32 devices in a mesh: dp: 4 (over y, x), expert: 8 (over z, core).
Axes of the slice: x: 2, y: 2, z: 4, core: 2. Of those that a mesh axis runs over, the one named last changes fastest.
Arguments:
- tokens: bfloat16 [4096, 7168], P(('dp', 'expert')), may hold values from -6 to 6
- cotangent: bfloat16 [4096, 7168], P(('dp', 'expert')), may hold values from -6 to 6
- route_ids: int32 [4096, 8], P(('dp', 'expert')), may hold values from 0 to 31, all different within a row; in each aligned block of 128 rows (0 to 127, 128 to 255, ...) at most 40 rows name the same one
- router_weights: float32 [4096, 8], P(('dp', 'expert')), may hold values from 0.05 to 0.3
- master: float32 [8, 7168, 384], P('expert', 'dp'), may hold values from -0.0625 to 0.0625
- accumulator: float32 [8, 3, 7168], P('expert', None, 'dp'), may hold values from 0.1 to 10
Outputs:
- output: bfloat16 [4096, 7168], P(('dp', 'expert'))
- input_grad: bfloat16 [4096, 7168], P(('dp', 'expert'))
- new_weights: bfloat16 [8, 7168, 384], P('expert', 'dp')
- accumulator_out: float32 [8, 3, 7168], P('expert', None, 'dp')
The draws below stay inside these ranges and needn't reach their ends.
Inputs may be any that keep to these rules, and one draw needn't show every extreme that they name: `route_ids`: each row names distinct experts. In each aligned block of 128 rows (the rows of one device) no expert is named by more than 40 rows, a bound that some block reaches.
All inputs are finite; a program needn't handle non-finite values.
Results may differ from the reference program's by a relative error of at most 0.011.
Values may be sent and summed in bfloat16 or wider, within the bound.
A program may use at most 128 MiB of HBM per device.

```python
import math
import jax
import jax.numpy as jnp
import numpy as np
from jax import lax

D = 7168
SLICES = 8
TOP = 8
TOK_DEV = 128
H_DEV = 128
EXPERTS = 32
GROUP = 1
SLOTS = 8
CAP = 40
TOKENS = 4096
N_DP = 4
N_EXPERT = 8


def level_of(key, dims, shards, least, high):
    def one(axis_at, shards_of):
        steps = jax.random.uniform(jax.random.fold_in(jax.random.fold_in(key, 6), axis_at), (shards_of,), jnp.float32, least / len(shards), high / len(shards))
        return jnp.repeat(jnp.exp(steps), dims[axis_at] // shards_of).reshape((-1,) + (1,) * (len(dims) - axis_at - 1))

    level = one(*shards[0])
    for cut in shards[1:]:
        level = level * one(*cut)
    return level


def assign_block(key, own, number, rows, count, top, limit, lean):
    order = jax.random.permutation(key, count)
    packed, common = shares(count, rows * top, limit, lean, True), shares(count, rows * top, limit, lean, False)
    places = jnp.arange(count)

    def named(lengths, offset_by):
        used = int((lengths > 0).sum())
        fixed = max(1, used // 4)
        shifted = fixed + (places - fixed + offset_by * (used - fixed)) % max(1, count - fixed)
        return jnp.zeros((count,), jnp.int32).at[order[jnp.where(places < fixed, places, shifted)]].set(jnp.asarray(lengths, jnp.int32))

    lengths = jnp.where(number % 4 == 0, named(packed, number // 4), named(common, number - number // 4 - 1))
    mixed = jax.random.permutation(jax.random.fold_in(own, 3), count)
    giver, taker = mixed[0:count // 2 * 2:2], mixed[1:count // 2 * 2:2]
    margin = jnp.minimum(lengths[giver] - 1, limit - lengths[taker]) // 2
    margin = jnp.where((giver == order[0]) | (taker == order[0]) | (lengths[taker] == 0), 0, jnp.maximum(margin, 0))
    shifted = jax.random.randint(jax.random.fold_in(own, 4), (count // 2,), 0, 1 << 20) % (margin + 1)
    lengths = lengths.at[giver].add(-shifted).at[taker].add(shifted)
    items = jnp.searchsorted(jnp.cumsum(lengths), jnp.arange(rows * top), side="right").astype(jnp.int32)
    table = items.reshape(top, rows).T
    table = table[jax.random.permutation(jax.random.fold_in(own, 1), rows)]
    offset_by = jax.random.randint(jax.random.fold_in(own, 2), (rows, 1), 0, top)
    return jnp.take_along_axis(table, (jnp.arange(top)[None, :] + offset_by) % top, axis=1)


def shares(number_of, total, bound, lean, full):
    portions = [(1 << 20) // math.isqrt(rank ** lean) + 1 for rank in range(1, number_of + 1)]
    largest = bound if full else min(bound, max(-(-total // number_of), total * portions[0] // sum(portions)))
    least = 1 if total - largest >= number_of - 1 else 0
    counts, rest = [largest] + [least] * (number_of - 1), total - largest - least * (number_of - 1)
    while rest > 0:
        candidates = [i for i in range(1, number_of) if counts[i] < largest] or [i for i in range(1, number_of) if counts[i] < bound]
        pool, remaining = sum([portions[i] for i in candidates]), rest
        for i in candidates:
            addition = min(bound - counts[i], max(1, remaining * portions[i] // pool), rest)
            counts[i] = counts[i] + addition
            rest = rest - addition
    return np.array(counts)


def bell_draw(stream_key, dims, deviation, bound, split=(), kind=jnp.bfloat16):
    entries = deviation * jax.random.normal(stream_key, dims, jnp.float32)
    if split:
        entries = entries * level_of(stream_key, dims, split, -0.22, 0.18)
    return jnp.clip(entries, -bound, bound).astype(kind)


def setup_inputs(seed: int = 0) -> dict:
    key_of = jax.random.split(jax.random.key(seed), 7)
    tokens = bell_draw(key_of[0], (TOKENS, D), 1.0, 6.0, ((0, 32),))
    cotangent = bell_draw(key_of[1], (TOKENS, D), 1.0, 6.0, ((0, 32),))
    route_ids_keys = jax.random.split(jax.random.fold_in(key_of[2], 1), TOKENS // TOK_DEV)
    route_ids_turns = jax.random.permutation(jax.random.fold_in(key_of[2], 3), TOKENS // TOK_DEV)
    route_ids = jax.vmap(lambda own, number: assign_block(jax.random.fold_in(key_of[2], 2), own, number, TOK_DEV, EXPERTS, TOP, CAP, 2))(route_ids_keys, route_ids_turns).reshape((TOKENS, TOP))
    router_weights = jnp.clip(0.05 + 0.25 * jax.random.uniform(key_of[3], (TOKENS, TOP), jnp.float32) ** level_of(key_of[3], (TOKENS, TOP), ((0, 32),), -0.2, 0.2), 0.05, 0.3)
    master = bell_draw(key_of[4], (SLOTS, D, 3 * H_DEV), D ** -0.5, 0.0625, ((0, 8), (1, 4)), jnp.float32)
    accumulator = jnp.clip(jnp.exp(math.log(10.0) - 4.6051702 * jax.random.uniform(key_of[5], (SLOTS, 3, D), jnp.float32) ** level_of(key_of[5], (SLOTS, 3, D), ((0, 8), (2, 4)), -0.2, 0.2)), 0.1, 10.0)
    return dict(tokens=tokens, cotangent=cotangent, route_ids=route_ids, router_weights=router_weights, master=master, accumulator=accumulator)


LEARN_RATE = 0.01
EPSILON = 1e-06

def slot_table(block_ids, live_count, capacity):
    flat_ids = block_ids.reshape(-1)
    onehot = (flat_ids[:, None] == jnp.arange(live_count, dtype=jnp.int32)[None, :]).astype(jnp.int32)
    before = jnp.cumsum(onehot, axis=0) - onehot
    position = lax.optimization_barrier(jnp.sum(before * onehot, axis=1))
    return jnp.where(flat_ids < live_count, flat_ids * capacity + position, live_count * capacity).astype(jnp.int32)

def pair_flip(array):
    shape = array.shape
    return array.reshape((shape[0] // 2, 2) + shape[1:])[:, ::-1].reshape(shape)

def expert_pass(operands):
    in_rows, cot_rows, slice_weights = operands
    hdev = H_DEV
    x_full = in_rows.astype(jnp.float32)
    d_full = cot_rows.astype(jnp.float32)
    w_full = slice_weights.astype(jnp.float32)
    high = lax.Precision.HIGHEST
    gate_up = jnp.einsum('rd,sdh->srh', x_full, w_full[:, :, :2 * hdev], precision=high)
    gate_pre = gate_up[:, :, :hdev]
    up_pre = gate_up[:, :, hdev:]
    sigmoid_gate = jax.nn.sigmoid(gate_pre)
    silu_gate = gate_pre * sigmoid_gate
    hidden = (silu_gate * up_pre).astype(jnp.bfloat16)
    hidden_full = hidden.astype(jnp.float32)
    down_cols = w_full[:, :, 2 * hdev:]
    out_part = jnp.einsum('srh,sdh->srd', hidden_full, down_cols, precision=high).astype(jnp.bfloat16)
    grad_hidden = jnp.einsum('rd,sdh->srh', d_full, down_cols, precision=high)
    grad_gate = grad_hidden * up_pre * sigmoid_gate * (1.0 + gate_pre * (1.0 - sigmoid_gate))
    grad_up = grad_hidden * silu_gate
    grad_pre = jnp.concatenate([grad_gate, grad_up], axis=2).astype(jnp.bfloat16)
    grad_full = grad_pre.astype(jnp.float32)
    in_part = jnp.einsum('srk,sdk->srd', grad_full, w_full[:, :, :2 * hdev], precision=high).astype(jnp.bfloat16)
    grad_in = jnp.einsum('rd,srk->sdk', x_full, grad_full, precision=high)
    grad_down = jnp.einsum('rd,srh->sdh', d_full, hidden_full, precision=high)
    replica_grad = jnp.concatenate([grad_in, grad_down], axis=2).astype(jnp.bfloat16)
    return (out_part, in_part, replica_grad)

def reference(tokens, cotangent, route_ids, router_weights, master, accumulator):
    devices_e = N_EXPERT
    tok_rows = TOK_DEV
    live_count = GROUP
    capacity = CAP
    hdev = H_DEV
    width = live_count * capacity
    working = pair_flip(master).astype(jnp.bfloat16).reshape(live_count, SLICES, D, 3 * hdev)
    total = jnp.zeros((SLOTS, D, 3 * hdev), jnp.float32)
    outputs = []
    in_grads = []
    device_rows = jnp.arange(devices_e, dtype=jnp.int32)[:, None]
    token_of = jnp.repeat(jnp.arange(tok_rows, dtype=jnp.int32), TOP)
    for replica in range(N_DP):
        start = replica * devices_e * tok_rows
        stop = start + devices_e * tok_rows
        x_rep = tokens[start:stop].reshape(devices_e, tok_rows, D)
        c_rep = cotangent[start:stop].reshape(devices_e, tok_rows, D)
        ids_rep = route_ids[start:stop].reshape(devices_e, tok_rows, TOP)
        w_rep = router_weights[start:stop].reshape(devices_e, tok_rows * TOP)
        slot_ids = jax.vmap(lambda block: slot_table(block, live_count, capacity))(ids_rep)
        source = jnp.broadcast_to(token_of[None, :], slot_ids.shape)
        index = jnp.zeros((devices_e, width), jnp.int32).at[device_rows, slot_ids].set(source, mode='drop')
        filled = jnp.zeros((devices_e, width), jnp.float32).at[device_rows, slot_ids].set(1.0, mode='drop')
        weight_slot = jnp.zeros((devices_e, width), jnp.float32).at[device_rows, slot_ids].set(w_rep, mode='drop')
        x_sel = jax.vmap(lambda rows, picks: rows[picks])(x_rep, index)
        c_sel = jax.vmap(lambda rows, picks: rows[picks])(c_rep, index)
        x_sel = jnp.where(filled[:, :, None] > 0, x_sel, jnp.zeros_like(x_sel))
        d_sel = (c_sel.astype(jnp.float32) * weight_slot[:, :, None]).astype(jnp.bfloat16)
        x_exp = x_sel.reshape(devices_e, live_count, capacity, D).transpose(1, 0, 2, 3).reshape(live_count, devices_e * capacity, D)
        d_exp = d_sel.reshape(devices_e, live_count, capacity, D).transpose(1, 0, 2, 3).reshape(live_count, devices_e * capacity, D)
        out_part, in_part, replica_grad = lax.map(expert_pass, (x_exp, d_exp, working))
        out_sum = lax.optimization_barrier(jnp.sum(out_part.astype(jnp.float32), axis=1))
        in_sum = lax.optimization_barrier(jnp.sum(in_part.astype(jnp.float32), axis=1))
        out_sum = out_sum.reshape(live_count, devices_e, capacity, D).transpose(1, 0, 2, 3).reshape(devices_e, width, D)
        in_sum = in_sum.reshape(live_count, devices_e, capacity, D).transpose(1, 0, 2, 3).reshape(devices_e, width, D)
        y_rep = jnp.zeros((devices_e, tok_rows, D), jnp.float32).at[device_rows, index].add(out_sum * weight_slot[:, :, None])
        dx_rep = jnp.zeros((devices_e, tok_rows, D), jnp.float32).at[device_rows, index].add(in_sum * filled[:, :, None])
        outputs.append(y_rep.reshape(devices_e * tok_rows, D).astype(jnp.bfloat16))
        in_grads.append(dx_rep.reshape(devices_e * tok_rows, D).astype(jnp.bfloat16))
        total = total + replica_grad.reshape(SLOTS, D, 3 * hdev).astype(jnp.float32)
    gradient = total.astype(jnp.bfloat16)
    grad_master = pair_flip(gradient).astype(jnp.float32).reshape(SLOTS, D, 3, hdev)
    mean_square = lax.optimization_barrier(jnp.mean(grad_master * grad_master, axis=3))
    accumulator_out = accumulator + mean_square.transpose(0, 2, 1)
    scale = 1.0 / (jnp.sqrt(accumulator_out) + EPSILON)
    update = grad_master * scale.transpose(0, 2, 1)[:, :, :, None]
    master_new = master - LEARN_RATE * update.reshape(SLOTS, D, 3 * hdev)
    new_weights = pair_flip(master_new).astype(jnp.bfloat16)
    output = jnp.concatenate(outputs, axis=0)
    input_grad = jnp.concatenate(in_grads, axis=0)
    return (output, input_grad, new_weights, accumulator_out)
```

```python
import jax
import jax.numpy as jnp
from jax import lax
from jax.sharding import Mesh
from jax.sharding import PartitionSpec as P

SLICES = 8
CORES = 2
EXP_DEV = 4

LEARN_RATE = 0.01
EPSILON = 1e-06


def swap(array):
    return lax.ppermute(array, "core", [(0, 1), (1, 0)])


def ordered(core, own, other, axis):
    first = jnp.where(core == 0, own, other)
    second = jnp.where(core == 0, other, own)
    return jnp.concatenate([first, second], axis=axis)


def slot_hits(block_ids, live_count, capacity):
    rows, top = block_ids.shape
    flat_ids = block_ids.reshape(-1)
    onehot = (flat_ids[:, None] == jnp.arange(live_count, dtype=jnp.int32)[None, :]).astype(
        jnp.int32
    )
    before = jnp.cumsum(onehot, axis=0) - onehot
    position = jnp.sum(before * onehot, axis=1)
    slots = jnp.where(flat_ids < live_count, flat_ids * capacity + position, live_count * capacity)
    slot_index = jnp.arange(live_count * capacity, dtype=jnp.int32)
    return slots.reshape(rows, top)[:, :, None] == slot_index[None, None, :]


def dot(left, right, left_dim, right_dim, precision=None):
    return lax.dot_general(
        left,
        right,
        (((left_dim,), (right_dim,)), ((), ())),
        preferred_element_type=jnp.float32,
        precision=precision,
    )


def local(tokens, cotangent, route_ids, router_weights, master, accumulator):
    devices_e = lax.axis_size("ex") * SLICES
    live_count = lax.axis_size("ex")
    chips = lax.axis_size("sl")
    replicas = lax.axis_size("dp")
    core = lax.axis_index("core")
    tok_rows = tokens.shape[0]
    model_width = tokens.shape[1]
    top = route_ids.shape[1]
    experts = EXP_DEV * devices_e
    capacity = max(2, 5 * tok_rows * top // (4 * experts))
    slice_width = master.shape[2] // 3
    quarter = master.shape[1]
    half = quarter // CORES
    width = live_count * capacity
    half_width = model_width // CORES
    bf16 = jnp.bfloat16

    def split_cols(rows):
        parts = rows.reshape(rows.shape[0], replicas, CORES, half)
        first = parts[:, :, 0].reshape(rows.shape[0], half_width)
        second = parts[:, :, 1].reshape(rows.shape[0], half_width)
        return jnp.where(core == 0, first, second), jnp.where(core == 0, second, first)

    def join_cols(own, other):
        first = jnp.where(core == 0, own, other)
        second = jnp.where(core == 0, other, own)
        shape = (own.shape[0], replicas, 1, half)
        return jnp.concatenate([first.reshape(shape), second.reshape(shape)], axis=2).reshape(
            own.shape[0], model_width
        )

    held = master[0].astype(bf16)
    held_low, held_high = held[:half], held[half:]
    held_mine = jnp.where(core == 0, held_low, held_high)
    held_other = jnp.where(core == 0, held_high, held_low)
    got = swap(held_other)
    slice_a = jnp.where(core == 0, got, held_mine)
    slice_b = jnp.where(core == 0, held_mine, got)
    two = 2 * slice_width
    paired = jnp.concatenate(
        [slice_a[:, :two], slice_b[:, :two], slice_a[:, two:], slice_b[:, two:]], axis=1
    )
    weights = lax.all_gather(paired, "dp", axis=0, tiled=True)
    w_in = weights[:, : 2 * two]
    w_down = weights[:, 2 * two :]

    picks = slot_hits(route_ids, live_count, capacity)
    hits = jnp.sum(picks.astype(jnp.float32), axis=1)
    slot_weight = jnp.sum(jnp.where(picks, router_weights[:, :, None], 0.0), axis=(0, 1))
    select = hits.astype(bf16)
    token_rows = dot(select, tokens, 0, 0).astype(bf16)
    grad_rows = (dot(select, cotangent, 0, 0) * slot_weight[:, None]).astype(bf16)

    def gather(rows):
        own, other = split_cols(rows)
        block = ordered(
            core,
            own.reshape(live_count, 1, capacity, half_width),
            swap(other).reshape(live_count, 1, capacity, half_width),
            1,
        )
        if live_count > 1:
            block = lax.all_to_all(block, "ex", split_axis=0, concat_axis=0, tiled=True)
        block = block.reshape(1, live_count * CORES * capacity, half_width)
        tiled = jnp.broadcast_to(block, (chips,) + block.shape[1:])
        full = lax.all_to_all(tiled, "sl", split_axis=0, concat_axis=0, tiled=True)
        return full.reshape(-1, half_width)

    def give_back(part):
        blocks = part.reshape(chips, live_count * CORES * capacity, half_width)
        back = lax.all_to_all(blocks, "sl", split_axis=0, concat_axis=0, tiled=True)
        summed = jnp.sum(back.astype(jnp.float32), axis=0).astype(bf16)
        summed = summed.reshape(live_count, CORES, capacity, half_width)
        if live_count > 1:
            summed = lax.all_to_all(summed, "ex", split_axis=0, concat_axis=0, tiled=True)
        low = summed[:, 0].reshape(width, half_width)
        high = summed[:, 1].reshape(width, half_width)
        own = jnp.where(core == 0, low, high)
        other = swap(jnp.where(core == 0, high, low))
        return join_cols(own, other)

    in_rows = gather(token_rows)
    cot_rows = gather(grad_rows)

    gate_up_part = dot(in_rows, w_in, 1, 0)
    gate_up = gate_up_part + swap(gate_up_part)
    gate_pre = jnp.concatenate(
        [gate_up[:, :slice_width], gate_up[:, two : two + slice_width]], axis=1
    )
    up_pre = jnp.concatenate(
        [gate_up[:, slice_width:two], gate_up[:, two + slice_width :]], axis=1
    )
    sigmoid_gate = jax.nn.sigmoid(gate_pre)
    silu_gate = gate_pre * sigmoid_gate
    hidden = (silu_gate * up_pre).astype(bf16)
    out_part = dot(hidden, w_down, 1, 1).astype(bf16)
    out_rows = give_back(out_part)

    grad_hidden_part = dot(cot_rows, w_down, 1, 0)
    grad_hidden = grad_hidden_part + swap(grad_hidden_part)
    grad_gate = grad_hidden * up_pre * sigmoid_gate * (1.0 + gate_pre * (1.0 - sigmoid_gate))
    grad_up = grad_hidden * silu_gate
    grad_pre = jnp.concatenate(
        [
            grad_gate[:, :slice_width],
            grad_up[:, :slice_width],
            grad_gate[:, slice_width:],
            grad_up[:, slice_width:],
        ],
        axis=1,
    ).astype(bf16)
    in_part = dot(grad_pre, w_in, 1, 1).astype(bf16)
    back_rows = give_back(in_part)

    grad_in = dot(in_rows, grad_pre, 0, 0).astype(bf16)
    grad_down = dot(cot_rows, hidden, 0, 0).astype(bf16)
    summed = lax.psum_scatter(
        jnp.concatenate([grad_in, grad_down], axis=1),
        "dp",
        scatter_dimension=0,
        tiled=True,
    )
    low = jnp.concatenate(
        [summed[:, :two], summed[:, 2 * two : 2 * two + slice_width]], axis=1
    )
    high = jnp.concatenate([summed[:, two : 2 * two], summed[:, 2 * two + slice_width :]], axis=1)
    mine = jnp.where(core == 0, high, low)
    theirs = swap(jnp.where(core == 0, low, high))
    held_grad = ordered(core, mine, theirs, 0)

    grad_full = held_grad.astype(jnp.float32).reshape(quarter, 3, slice_width)
    mean_square = jnp.mean(grad_full * grad_full, axis=2)
    accumulator_out = accumulator[0] + mean_square.T
    scale = 1.0 / (jnp.sqrt(accumulator_out) + EPSILON)
    update = grad_full * scale.T[:, :, None]
    master_new = master[0] - LEARN_RATE * update.reshape(quarter, 3 * slice_width)
    returned = swap(master_new.astype(bf16))

    high_precision = lax.Precision.HIGHEST
    output = dot(
        hits * slot_weight[None, :], out_rows.astype(jnp.float32), 1, 0, high_precision
    ).astype(bf16)
    input_grad = dot(select, back_rows, 1, 0).astype(bf16)
    return (output, input_grad, returned[None], accumulator_out[None])


def solution(mesh):
    replicas, devices_e = mesh.devices.shape
    fine = Mesh(
        mesh.devices.reshape(replicas, devices_e // SLICES, SLICES // CORES, CORES),
        ("dp", "ex", "sl", "core"),
    )
    expert = ("ex", "sl", "core")
    rows = P(("dp",) + expert, None)
    return jax.shard_map(
        local,
        mesh=fine,
        in_specs=(rows, rows, rows, rows, P(expert, "dp", None), P(expert, None, "dp")),
        out_specs=(rows, rows, P(expert, "dp", None), P(expert, None, "dp")),
        check_vma=False,
    )
```

```python
import functools

import jax
import jax.numpy as jnp
from jax import lax
from jax.experimental import pallas as pl
from jax.experimental.pallas import tpu as pltpu
from jax.sharding import Mesh
from jax.sharding import PartitionSpec as P

SLICES = 8
CORES = 2
EXP_DEV = 4

LEARN_RATE = 0.01
EPSILON = 1e-06


def swap(array):
    return lax.ppermute(array, "core", [(0, 1), (1, 0)])


def ordered(core, own, other, axis):
    first = jnp.where(core == 0, own, other)
    second = jnp.where(core == 0, other, own)
    return jnp.concatenate([first, second], axis=axis)


def slot_hits(block_ids, live_count, capacity):
    rows, top = block_ids.shape
    flat_ids = block_ids.reshape(-1)
    onehot = (flat_ids[:, None] == jnp.arange(live_count, dtype=jnp.int32)[None, :]).astype(
        jnp.int32
    )
    before = jnp.cumsum(onehot, axis=0) - onehot
    position = jnp.sum(before * onehot, axis=1)
    slots = jnp.where(flat_ids < live_count, flat_ids * capacity + position, live_count * capacity)
    slot_index = jnp.arange(live_count * capacity, dtype=jnp.int32)
    return slots.reshape(rows, top)[:, :, None] == slot_index[None, None, :]


def dot(left, right, left_dim, right_dim, precision=None):
    return lax.dot_general(
        left,
        right,
        (((left_dim,), (right_dim,)), ((), ())),
        preferred_element_type=jnp.float32,
        precision=precision,
    )


def greet_line(me, chips):
    barrier = pltpu.get_barrier_semaphore()
    for cond, peer in ((me < chips - 1, me + 1), (me > 0, me - 1)):

        @pl.when(cond)
        def _():
            pl.semaphore_signal(
                barrier,
                inc=1,
                device_id={"sl": peer},
                device_id_type=pl.DeviceIdType.MESH,
            )

    inner = (me > 0) & (me < chips - 1)
    pl.semaphore_wait(barrier, jnp.where(inner, 2, 1))


def gather_kernel(chips, *refs):
    count = (len(refs) - 3) // 2
    blocks, outs = refs[:count], refs[count : 2 * count]
    own_sem, send_sem, recv_sem = refs[2 * count :]
    me = lax.axis_index("sl")
    greet_line(me, chips)

    def copy(way, part, hop, source):
        step = 1 - 2 * way
        index = me - step * hop
        return pltpu.make_async_remote_copy(
            src_ref=source if source is not None else outs[part].at[index],
            dst_ref=outs[part].at[index],
            send_sem=send_sem.at[way, part, hop],
            recv_sem=recv_sem.at[way, part, hop],
            device_id={"sl": me + step},
            device_id_type=pl.DeviceIdType.MESH,
        )

    def arrival(way, part, hop):
        step = 1 - 2 * way
        index = me - step * (hop + 1)
        return pltpu.make_async_remote_copy(
            src_ref=outs[part].at[index],
            dst_ref=outs[part].at[index],
            send_sem=send_sem.at[way, part, hop],
            recv_sem=recv_sem.at[way, part, hop],
            device_id={"sl": me - step},
            device_id_type=pl.DeviceIdType.MESH,
        )

    def place(way):
        return me if way == 0 else chips - 1 - me

    for part in range(count):
        for way in range(2):

            @pl.when(place(way) < chips - 1)
            def _():
                copy(way, part, 0, blocks[part]).start()

    owns = []
    for part in range(count):
        own = pltpu.make_async_copy(blocks[part], outs[part].at[me], own_sem.at[part])
        own.start()
        owns.append(own)
    for hop in range(1, chips):
        for part in range(count):
            for way in range(2):

                @pl.when(place(way) >= hop)
                def _():
                    arrival(way, part, hop - 1).wait_recv()

                if hop < chips - 1:

                    @pl.when((place(way) >= hop) & (place(way) < chips - 1))
                    def _():
                        copy(way, part, hop, None).start()

    for own in owns:
        own.wait()
    for hop in range(chips - 1):
        for part in range(count):
            for way in range(2):

                @pl.when((place(way) >= hop) & (place(way) < chips - 1))
                def _():
                    copy(way, part, hop, blocks[part] if hop == 0 else None).wait_send()


def line_gather(chips, blocks):
    rows, columns = blocks[0].shape
    count = len(blocks)
    return pl.pallas_call(
        functools.partial(gather_kernel, chips),
        out_shape=[jax.ShapeDtypeStruct((chips, rows, columns), b.dtype) for b in blocks],
        in_specs=[pl.BlockSpec(memory_space=pltpu.VMEM)] * count,
        out_specs=[pl.BlockSpec(memory_space=pl.ANY)] * count,
        scratch_shapes=[
            pltpu.SemaphoreType.DMA((count,)),
            pltpu.SemaphoreType.DMA((2, count, chips - 1)),
            pltpu.SemaphoreType.DMA((2, count, chips - 1)),
        ],
        compiler_params=pltpu.CompilerParams(collective_id=0, has_side_effects=True),
        name="line_gather",
    )(*blocks)


def reduce_kernel(chips, *refs):
    count = (len(refs) - 4) // 2
    parts, outs = refs[:count], refs[count : 2 * count]
    landed, sums, send_sem, recv_sem = refs[2 * count :]
    me = lax.axis_index("sl")
    greet_line(me, chips)

    def place(way):
        return me if way == 0 else chips - 1 - me

    def target(way, slot):
        return chips - 1 - slot if way == 0 else slot

    def copy(way, part, slot, source):
        return pltpu.make_async_remote_copy(
            src_ref=source,
            dst_ref=landed.at[way, part, slot],
            send_sem=send_sem.at[way, part, slot],
            recv_sem=recv_sem.at[way, part, slot],
            device_id={"sl": me + 1 - 2 * way},
            device_id_type=pl.DeviceIdType.MESH,
        )

    def arrival(way, part, slot):
        return pltpu.make_async_remote_copy(
            src_ref=landed.at[way, part, slot],
            dst_ref=landed.at[way, part, slot],
            send_sem=send_sem.at[way, part, slot],
            recv_sem=recv_sem.at[way, part, slot],
            device_id={"sl": me - 1 + 2 * way},
            device_id_type=pl.DeviceIdType.MESH,
        )

    for slot in range(chips - 1):
        for part in range(count):
            for way in range(2):

                @pl.when(place(way) == 0)
                def _():
                    copy(way, part, slot, parts[part].at[target(way, slot)]).start()

    for slot in range(chips - 2):
        for part in range(count):
            for way in range(2):

                @pl.when((place(way) > 0) & (place(way) < chips - 1 - slot))
                def _():
                    arrival(way, part, slot).wait_recv()
                    sums[way, part, slot] = (
                        landed[way, part, slot].astype(jnp.float32)
                        + parts[part][target(way, slot)].astype(jnp.float32)
                    ).astype(sums.dtype)
                    copy(way, part, slot, sums.at[way, part, slot]).start()

    for part in range(count):
        for here in range(chips):

            @pl.when(me == here)
            def _():
                total = parts[part][here].astype(jnp.float32)
                if here > 0:
                    arrival(0, part, chips - 1 - here).wait_recv()
                    total = total + landed[0, part, chips - 1 - here].astype(jnp.float32)
                if here < chips - 1:
                    arrival(1, part, here).wait_recv()
                    total = total + landed[1, part, here].astype(jnp.float32)
                outs[part][...] = total.astype(outs[part].dtype)

    for slot in range(chips - 1):
        for part in range(count):
            for way in range(2):

                @pl.when(place(way) == 0)
                def _():
                    copy(way, part, slot, parts[part].at[target(way, slot)]).wait_send()

                if slot < chips - 2:

                    @pl.when((place(way) > 0) & (place(way) < chips - 1 - slot))
                    def _():
                        copy(way, part, slot, sums.at[way, part, slot]).wait_send()


def line_reduce(chips, parts):
    _, rows, columns = parts[0].shape
    count = len(parts)
    kind = parts[0].dtype
    return pl.pallas_call(
        functools.partial(reduce_kernel, chips),
        out_shape=[jax.ShapeDtypeStruct((rows, columns), kind)] * count,
        in_specs=[pl.BlockSpec(memory_space=pltpu.VMEM)] * count,
        out_specs=[pl.BlockSpec(memory_space=pltpu.VMEM)] * count,
        scratch_shapes=[
            pltpu.VMEM((2, count, chips - 1, rows, columns), kind),
            pltpu.VMEM((2, count, chips - 2, rows, columns), kind),
            pltpu.SemaphoreType.DMA((2, count, chips - 1)),
            pltpu.SemaphoreType.DMA((2, count, chips - 1)),
        ],
        compiler_params=pltpu.CompilerParams(
            collective_id=1, has_side_effects=True, vmem_limit_bytes=48 * 1024 * 1024
        ),
        name="line_reduce",
    )(*parts)


def local(tokens, cotangent, route_ids, router_weights, master, accumulator):
    devices_e = lax.axis_size("ex") * SLICES
    live_count = lax.axis_size("ex")
    chips = lax.axis_size("sl")
    replicas = lax.axis_size("dp")
    core = lax.axis_index("core")
    tok_rows = tokens.shape[0]
    model_width = tokens.shape[1]
    top = route_ids.shape[1]
    experts = EXP_DEV * devices_e
    capacity = max(2, 5 * tok_rows * top // (4 * experts))
    slice_width = master.shape[2] // 3
    quarter = master.shape[1]
    half = quarter // CORES
    width = live_count * capacity
    half_width = model_width // CORES
    bf16 = jnp.bfloat16

    def split_cols(rows):
        parts = rows.reshape(rows.shape[0], replicas, CORES, half)
        first = parts[:, :, 0].reshape(rows.shape[0], half_width)
        second = parts[:, :, 1].reshape(rows.shape[0], half_width)
        return jnp.where(core == 0, first, second), jnp.where(core == 0, second, first)

    def join_cols(own, other):
        first = jnp.where(core == 0, own, other)
        second = jnp.where(core == 0, other, own)
        shape = (own.shape[0], replicas, 1, half)
        return jnp.concatenate([first.reshape(shape), second.reshape(shape)], axis=2).reshape(
            own.shape[0], model_width
        )

    held = master[0].astype(bf16)
    held_low, held_high = held[:half], held[half:]
    held_mine = jnp.where(core == 0, held_low, held_high)
    held_other = jnp.where(core == 0, held_high, held_low)
    got = swap(held_other)
    slice_a = jnp.where(core == 0, got, held_mine)
    slice_b = jnp.where(core == 0, held_mine, got)
    two = 2 * slice_width
    paired = jnp.concatenate(
        [slice_a[:, :two], slice_b[:, :two], slice_a[:, two:], slice_b[:, two:]], axis=1
    )
    weights = lax.all_gather(paired, "dp", axis=0, tiled=True)
    w_in = weights[:, : 2 * two]
    w_down = weights[:, 2 * two :]

    picks = slot_hits(route_ids, live_count, capacity)
    hits = jnp.sum(picks.astype(jnp.float32), axis=1)
    slot_weight = jnp.sum(jnp.where(picks, router_weights[:, :, None], 0.0), axis=(0, 1))
    select = hits.astype(bf16)
    token_rows = dot(select, tokens, 0, 0).astype(bf16)
    grad_rows = (dot(select, cotangent, 0, 0) * slot_weight[:, None]).astype(bf16)

    def pair_block(rows):
        own, other = split_cols(rows)
        block = ordered(
            core,
            own.reshape(live_count, 1, capacity, half_width),
            swap(other).reshape(live_count, 1, capacity, half_width),
            1,
        )
        if live_count > 1:
            block = lax.all_to_all(block, "ex", split_axis=0, concat_axis=0, tiled=True)
        return block.reshape(live_count * CORES * capacity, half_width)

    def give_back(summed):
        summed = summed.reshape(live_count, CORES, capacity, half_width)
        if live_count > 1:
            summed = lax.all_to_all(summed, "ex", split_axis=0, concat_axis=0, tiled=True)
        low = summed[:, 0].reshape(width, half_width)
        high = summed[:, 1].reshape(width, half_width)
        own = jnp.where(core == 0, low, high)
        other = swap(jnp.where(core == 0, high, low))
        return join_cols(own, other)

    in_rows, cot_rows = line_gather(chips, [pair_block(token_rows), pair_block(grad_rows)])
    in_rows = in_rows.reshape(-1, half_width)
    cot_rows = cot_rows.reshape(-1, half_width)

    gate_up_part = dot(in_rows, w_in, 1, 0)
    gate_up = gate_up_part + swap(gate_up_part)
    gate_pre = jnp.concatenate(
        [gate_up[:, :slice_width], gate_up[:, two : two + slice_width]], axis=1
    )
    up_pre = jnp.concatenate(
        [gate_up[:, slice_width:two], gate_up[:, two + slice_width :]], axis=1
    )
    sigmoid_gate = jax.nn.sigmoid(gate_pre)
    silu_gate = gate_pre * sigmoid_gate
    hidden = (silu_gate * up_pre).astype(bf16)
    out_part = dot(hidden, w_down, 1, 1).astype(bf16)

    grad_hidden_part = dot(cot_rows, w_down, 1, 0)
    grad_hidden = grad_hidden_part + swap(grad_hidden_part)
    grad_gate = grad_hidden * up_pre * sigmoid_gate * (1.0 + gate_pre * (1.0 - sigmoid_gate))
    grad_up = grad_hidden * silu_gate
    grad_pre = jnp.concatenate(
        [
            grad_gate[:, :slice_width],
            grad_up[:, :slice_width],
            grad_gate[:, slice_width:],
            grad_up[:, slice_width:],
        ],
        axis=1,
    ).astype(bf16)
    in_part = dot(grad_pre, w_in, 1, 1).astype(bf16)

    grad_in = dot(in_rows, grad_pre, 0, 0).astype(bf16)
    grad_down = dot(cot_rows, hidden, 0, 0).astype(bf16)
    summed = lax.psum_scatter(
        jnp.concatenate([grad_in, grad_down], axis=1),
        "dp",
        scatter_dimension=0,
        tiled=True,
    )
    blocks = (chips, live_count * CORES * capacity, half_width)
    out_sum, in_sum = line_reduce(chips, [out_part.reshape(blocks), in_part.reshape(blocks)])
    out_rows = give_back(out_sum)
    back_rows = give_back(in_sum)
    low = jnp.concatenate(
        [summed[:, :two], summed[:, 2 * two : 2 * two + slice_width]], axis=1
    )
    high = jnp.concatenate([summed[:, two : 2 * two], summed[:, 2 * two + slice_width :]], axis=1)
    mine = jnp.where(core == 0, high, low)
    theirs = swap(jnp.where(core == 0, low, high))
    held_grad = ordered(core, mine, theirs, 0)

    grad_full = held_grad.astype(jnp.float32).reshape(quarter, 3, slice_width)
    mean_square = jnp.mean(grad_full * grad_full, axis=2)
    accumulator_out = accumulator[0] + mean_square.T
    scale = 1.0 / (jnp.sqrt(accumulator_out) + EPSILON)
    update = grad_full * scale.T[:, :, None]
    master_new = master[0] - LEARN_RATE * update.reshape(quarter, 3 * slice_width)
    returned = swap(master_new.astype(bf16))

    high_precision = lax.Precision.HIGHEST
    output = dot(
        hits * slot_weight[None, :], out_rows.astype(jnp.float32), 1, 0, high_precision
    ).astype(bf16)
    input_grad = dot(select, back_rows, 1, 0).astype(bf16)
    return (output, input_grad, returned[None], accumulator_out[None])


def solution(mesh):
    replicas, devices_e = mesh.devices.shape
    fine = Mesh(
        mesh.devices.reshape(replicas, devices_e // SLICES, SLICES // CORES, CORES),
        ("dp", "ex", "sl", "core"),
    )
    expert = ("ex", "sl", "core")
    rows = P(("dp",) + expert, None)
    return jax.shard_map(
        local,
        mesh=fine,
        in_specs=(rows, rows, rows, rows, P(expert, "dp", None), P(expert, None, "dp")),
        out_specs=(rows, rows, P(expert, "dp", None), P(expert, None, "dp")),
        check_vma=False,
    )
```
